1024 devices in a mesh: dir: 32 (over z, x_lo), slab: 32 (over y, x_hi, core).
Axes of the slice: x: 8 (x_hi: 2, x_lo: 4; x = x_hi * 4 + x_lo), y: 8, z: 8, core: 2. Of those that a mesh axis runs over, the one named last changes fastest.
Arguments:
- child_fields: bfloat16 [64, 32, 2, 8, 2, 2, 512], P('slab', 'dir'), may hold values from -6 to 6
- occupancy: int32 [64, 32, 2], P('slab', 'dir'), may hold values 0 or 1
- child_octant: int32 [64, 32, 2, 8], P('slab', 'dir'), may hold values from 0 to 7, each once within a row
- shift_angle: float32 [8, 2048], replicated, may hold values from -3.140625 to 3.140625
- interp_matrix: bfloat16 [512, 2048], replicated, may hold values from -0.25 to 0.25
- trans_table: float32 [7, 7, 7, 2, 2048], P(None, None, None, None, 'dir'), may hold values from -0.2 to 0.2
- impedance: float32 [64, 32, 2, 8, 2], P('slab', 'dir'), may hold values from -4 to 4
Outputs:
- child_incoming: bfloat16 [64, 32, 2, 8, 2, 2, 512], P('slab', 'dir')
The draws below stay inside these ranges and needn't reach their ends.
Inputs may be any that keep to these rules, and one draw needn't show every extreme that they name: `child_octant`: the 8 child slots of every parent box name the 8 octants once each.
All inputs are finite; a program needn't handle non-finite values. No bound on the sum of `occupancy` on one device may be relied on, other than what follows from the above.
Results may differ from the reference program's by a relative error of at most 0.0064.
Values may be sent and summed in bfloat16 or wider, within the bound.
A program may use at most 128 MiB of HBM per device.

```python
import jax
import jax.numpy as jnp
from jax import lax

KC = 512
KP = 2048
EXC = 2
GZ = 2
GX = 64
GY = 32


def with_ends(entries, stream_key, low, largest):
    longest = entries.shape.index(max(entries.shape))
    spots = []
    for shift in (0, 1):
        where = [jax.random.randint(jax.random.fold_in(stream_key, axis), (), 0, length) for axis, length in enumerate(entries.shape)]
        where[longest] = (where[longest] + shift) % entries.shape[longest]
        spots.append(tuple(where))
    return entries.at[spots[0]].set(low).at[spots[1]].set(largest)


def shard_levels(key, shape, cuts, low, top_value):
    factor_of, own = 1.0, jax.random.fold_in(key, 6)
    for dim, blocks in cuts:
        steps = jnp.exp(jax.random.uniform(jax.random.fold_in(own, dim), (blocks,), jnp.float32, low / len(cuts), top_value / len(cuts)))
        factor_of = factor_of * jnp.repeat(steps, shape[dim] // blocks).reshape([-1 if axis == dim else 1 for axis in range(len(shape))])
    return factor_of


def centred(key, dims, scale, bound, shards=(), kind=jnp.bfloat16):
    values = scale * jax.random.normal(key, dims, jnp.float32)
    if shards:
        values = values * shard_levels(key, dims, shards, -0.22, 0.18)
    return jnp.clip(values, -bound, bound).astype(kind)


def setup_inputs(seed: int = 0) -> dict:
    streams_of = jax.random.split(jax.random.key(seed), 8)
    child_fields = centred(streams_of[0], (GX, GY, GZ, 8, EXC, 2, KC), 1.0, 6.0, ((0, 32), (1, 32)))
    occupancy = with_ends((jax.random.randint(streams_of[1], (GX, GY, GZ), 0, 4) < 3).astype(jnp.int32), jax.random.fold_in(streams_of[1], 1), 0, 1)
    child_octant = jax.vmap(lambda own: jax.random.permutation(own, 8))(jax.random.split(streams_of[2], GX * GY * GZ)).reshape((GX, GY, GZ, 8)).astype(jnp.int32)
    shift_angle = jnp.clip(jax.random.uniform(streams_of[3], (8, KP), jnp.float32, -3.140625, 3.140625), -3.140625, 3.140625)
    interp_matrix = centred(streams_of[4], (KC, KP), KC ** -0.5, 0.25)
    trans_table = centred(streams_of[5], (7, 7, 7, 2, KP), 0.04, 0.2, ((4, 32),), jnp.float32)
    impedance = centred(streams_of[6], (GX, GY, GZ, 8, 2), 1.0, 4.0, ((0, 32), (1, 32)), jnp.float32)
    return {"child_fields": child_fields, "occupancy": occupancy, "child_octant": child_octant, "shift_angle": shift_angle, "interp_matrix": interp_matrix, "trans_table": trans_table, "impedance": impedance}


def aggregate(spread, cos_rows, sin_rows, occupied):
    real_part = spread[..., 0, :]
    imag_part = spread[..., 1, :]
    cos_part = cos_rows[..., :, None, :]
    sin_part = sin_rows[..., :, None, :]
    real_sum = jnp.sum(cos_part * real_part - sin_part * imag_part, axis=-3)
    imag_sum = jnp.sum(cos_part * imag_part + sin_part * real_part, axis=-3)
    return jnp.stack([real_sum, imag_sum], axis=-2) * occupied[..., None, None, None]


def disaggregate(incoming, cos_rows, sin_rows):
    in_real = incoming[..., 0, :].astype(jnp.float32)[..., None, :, :]
    in_imag = incoming[..., 1, :].astype(jnp.float32)[..., None, :, :]
    cos_part = cos_rows[..., :, None, :]
    sin_part = sin_rows[..., :, None, :]
    real_out = cos_part * in_real + sin_part * in_imag
    imag_out = cos_part * in_imag - sin_part * in_real
    return jnp.stack([real_out, imag_out], axis=-2)


def impede(fields, impedance):
    imp_real = impedance[..., 0][..., None, None]
    imp_imag = impedance[..., 1][..., None, None]
    field_real = fields[..., 0, :]
    field_imag = fields[..., 1, :]
    return jnp.stack([imp_real * field_real - imp_imag * field_imag,
                      imp_real * field_imag + imp_imag * field_real], axis=-2)


def translate_strided(block_fields, block_table, count_x, count_y, count_z):
    shape_out = (count_x, count_y, count_z) + block_fields.shape[3:]
    result = jnp.zeros(shape_out, jnp.float32)
    for parity_x in range(2):
        for parity_y in range(2):
            for parity_z in range(2):
                real_sum = jnp.zeros((count_x // 2, count_y // 2, count_z // 2) + block_fields.shape[3:4] + block_fields.shape[5:], jnp.float32)
                imag_sum = real_sum
                for step_x in range(-2 - parity_x, 4 - parity_x):
                    for step_y in range(-2 - parity_y, 4 - parity_y):
                        if abs(step_y) >= count_y:
                            continue
                        for step_z in range(-2 - parity_z, 4 - parity_z):
                            if abs(step_z) >= count_z:
                                continue
                            if max(abs(step_x), abs(step_y), abs(step_z)) <= 1:
                                continue
                            start_x = 3 + parity_x + step_x
                            start_y = 3 + parity_y + step_y
                            start_z = 3 + parity_z + step_z
                            source_cells = block_fields[start_x:start_x + count_x:2, start_y:start_y + count_y:2, start_z:start_z + count_z:2].astype(jnp.float32)
                            real_part = source_cells[..., 0, :]
                            imag_part = source_cells[..., 1, :]
                            factor = block_table[step_x + 3, step_y + 3, step_z + 3]
                            real_sum = real_sum + factor[0] * real_part - factor[1] * imag_part
                            imag_sum = imag_sum + factor[0] * imag_part + factor[1] * real_part
                result = result.at[parity_x::2, parity_y::2, parity_z::2].set(jnp.stack([real_sum, imag_sum], axis=-2))
    return result.astype(jnp.bfloat16)


def translate_all(parent, trans_table):
    count_x, count_y, count_z = parent.shape[0], parent.shape[1], parent.shape[2]
    block_width = min(KP, 256)
    blocks = KP // block_width
    padded = jnp.pad(parent, ((3, 3), (3, 3), (3, 3), (0, 0), (0, 0), (0, 0)))
    padded = jnp.moveaxis(padded.reshape(padded.shape[:-1] + (blocks, block_width)), -2, 0)
    table_blocks = jnp.moveaxis(trans_table.reshape(trans_table.shape[:-1] + (blocks, block_width)), -2, 0)

    def one_block(packed):
        return translate_strided(packed[0], packed[1], count_x, count_y, count_z)

    result = lax.map(one_block, (padded, table_blocks))
    result = jnp.moveaxis(result, 0, -2)
    return result.reshape(result.shape[:-2] + (KP,))


def reference(child_fields, occupancy, child_octant, shift_angle, interp_matrix, trans_table, impedance):
    cos_table = jnp.cos(shift_angle)
    sin_table = jnp.sin(shift_angle)
    anterp_scale = (KC / KP) ** 0.5

    def upward(packed):
        row_fields, row_occupancy, row_octant = packed
        spread = jnp.dot(row_fields.reshape(-1, KC), interp_matrix, preferred_element_type=jnp.float32)
        spread = spread.reshape(row_fields.shape[:-1] + (KP,))
        summed = aggregate(spread, cos_table[row_octant], sin_table[row_octant], row_occupancy.astype(jnp.float32))
        return summed.astype(jnp.bfloat16)

    parent = lax.map(upward, (child_fields, occupancy, child_octant))
    incoming = translate_all(parent, trans_table)

    def downward(packed):
        row_incoming, row_octant, row_impedance = packed
        split = disaggregate(row_incoming, cos_table[row_octant], sin_table[row_octant]).astype(jnp.bfloat16)
        gathered = lax.dot_general(split.reshape(-1, KP), interp_matrix, (((1,), (1,)), ((), ())), preferred_element_type=jnp.float32) * anterp_scale
        gathered = gathered.reshape(split.shape[:-1] + (KC,))
        return impede(gathered, row_impedance).astype(jnp.bfloat16)

    return lax.map(downward, (incoming, child_octant, impedance))
```

```python
import functools

import jax
import jax.numpy as jnp
from jax import lax
from jax.experimental import pallas as pl
from jax.experimental.pallas import tpu as pltpu
from jax.sharding import PartitionSpec as P

MESH = pl.DeviceIdType.MESH
F32 = jnp.float32
BF16 = jnp.bfloat16


def lane_low(shape):
    return lax.broadcasted_iota(jnp.int32, shape, 1) < 64


def fused(
    n_dir, n_slab, scale,
    x_ref, occ_ref, oct_ref, ang_hbm, interp_hbm, table_hbm, imp_ref,
    out_ref,
    ang, interp, table, cos_t, sin_t, select, selectf, imp_cols, spread, send1, recv1,
    factors, field, totals, flat, send2, recv2, split,
    local_sem, send1_sem, recv1_sem, send2_sem, recv2_sem,
):
    d = lax.axis_index("dir")
    s = lax.axis_index("slab")
    not_first = s > 0
    not_last = s < n_slab - 1

    barrier = pltpu.get_barrier_semaphore()

    @pl.loop(0, n_dir)
    def _(k):
        t = lax.rem(d + k, n_dir)

        @pl.when(not_first)
        def _():
            pl.semaphore_signal(barrier, inc=1, device_id={"dir": t, "slab": s - 1}, device_id_type=MESH)

        @pl.when(not_last)
        def _():
            pl.semaphore_signal(barrier, inc=1, device_id={"dir": t, "slab": s + 1}, device_id_type=MESH)

        @pl.when(k > 0)
        def _():
            pl.semaphore_signal(barrier, inc=1, device_id={"dir": t, "slab": s}, device_id_type=MESH)

    load_ang = pltpu.make_async_copy(ang_hbm, ang, local_sem.at[0])
    load_interp = pltpu.make_async_copy(interp_hbm, interp, local_sem.at[1])
    load_table = pltpu.make_async_copy(table_hbm.at[:, :, 2:5], table, local_sem.at[2])
    load_ang.start()
    load_interp.start()
    load_table.start()

    lane = lax.broadcasted_iota(jnp.int32, (1, 128), 1)
    oct_lane = jnp.zeros((1, 128), jnp.int32)
    occ_lane = jnp.zeros((1, 128), F32)
    imp_re = jnp.zeros((1, 128), F32)
    imp_im = jnp.zeros((1, 128), F32)
    for box in range(4):
        x, z = box // 2, box % 2
        occ_lane = jnp.where(lane // 32 == box, occ_ref[x, 0, z].astype(F32), occ_lane)
        for slot in range(8):
            here = lane // 4 == box * 8 + slot
            oct_lane = jnp.where(here, oct_ref[x, 0, z, slot], oct_lane)
            imp_re = jnp.where(here, imp_ref[x, 0, z, slot, 0], imp_re)
            imp_im = jnp.where(here, imp_ref[x, 0, z, slot, 1], imp_im)
    row16 = lax.broadcasted_iota(jnp.int32, (16, 128), 0)
    lane16 = lax.broadcasted_iota(jnp.int32, (16, 128), 1)
    same = (row16 // 8 == (lane16 // 2) % 2) & ((row16 // 4) % 2 == lane16 % 2) & (row16 % 4 == lane16 // 32)
    for q in range(8):
        picked = jnp.where(same & (oct_lane == q), 1.0, 0.0).astype(F32)
        selectf[q * 16 : q * 16 + 16, :] = picked
        select[q * 16 : q * 16 + 16, :] = (picked * occ_lane).astype(BF16)
        imp_cols[0, q * 16 : q * 16 + 16, :] = jnp.broadcast_to(jnp.sum(picked * imp_re, axis=1, keepdims=True), (16, 128))
        imp_cols[1, q * 16 : q * 16 + 16, :] = jnp.broadcast_to(jnp.sum(picked * imp_im, axis=1, keepdims=True), (16, 128))

    sorted_x = jnp.dot(select[...], x_ref[...], preferred_element_type=F32).astype(BF16)
    load_ang.wait()
    cos_t[...] = jnp.cos(ang[...])
    sin_t[...] = jnp.sin(ang[...])
    load_interp.wait()
    spread[...] = jnp.dot(sorted_x, interp[...], preferred_element_type=F32)

    low8 = lane_low((8, 128))
    real8 = lax.broadcasted_iota(jnp.int32, (8, 128), 0) < 4
    up_sign = jnp.where(real8, -1.0, 1.0).astype(F32)
    down_sign = jnp.where(real8, 1.0, -1.0).astype(F32)

    @pl.loop(0, n_dir // 2)
    def _(j):
        cols = pl.ds(pl.multiple_of(j * 128, 128), 128)
        parts = []
        for e in range(2):
            straight = jnp.zeros((8, 128), F32)
            crossed = jnp.zeros((8, 128), F32)
            for q in range(8):
                v = spread[q * 16 + e * 8 : q * 16 + e * 8 + 8, cols]
                straight += cos_t[q : q + 1, cols] * v
                crossed += sin_t[q : q + 1, cols] * v
            parts.append(straight + up_sign * pltpu.roll(crossed, 4, 0))
        e0, e1 = parts
        send1[2 * j] = jnp.where(low8, e0, pltpu.roll(e1, 64, 1)).astype(BF16)
        send1[2 * j + 1] = jnp.where(low8, pltpu.roll(e0, 64, 1), e1).astype(BF16)

    pl.semaphore_wait(
        barrier,
        n_dir - 1 + n_dir * not_first.astype(jnp.int32) + n_dir * not_last.astype(jnp.int32),
    )

    @pl.loop(0, n_dir)
    def _(k):
        t = lax.rem(d + k, n_dir)

        @pl.when(not_first)
        def _():
            pltpu.make_async_remote_copy(
                send1.at[t], recv1.at[2, d], send1_sem.at[0], recv1_sem.at[2],
                device_id={"dir": t, "slab": s - 1}, device_id_type=MESH,
            ).start()

        @pl.when(not_last)
        def _():
            pltpu.make_async_remote_copy(
                send1.at[t], recv1.at[0, d], send1_sem.at[2], recv1_sem.at[0],
                device_id={"dir": t, "slab": s + 1}, device_id_type=MESH,
            ).start()

        @pl.when(k > 0)
        def _():
            pltpu.make_async_remote_copy(
                send1.at[t], recv1.at[1, d], send1_sem.at[1], recv1_sem.at[1],
                device_id={"dir": t, "slab": s}, device_id_type=MESH,
            ).start()

    pltpu.make_async_copy(send1.at[d], recv1.at[1, d], recv1_sem.at[1]).start()

    load_table.wait()

    @pl.loop(0, 49)
    def _(i):
        a, b = i // 7, i % 7
        for c in range(3):
            for part in range(2):
                row = table[a, b, c, part : part + 1, :]
                both = jnp.concatenate([row, row], axis=1)
                factors[i * 6 + c * 2 + part] = jnp.broadcast_to(both, (8, 128))

    field[0:16, :] = jnp.zeros((16, 128), F32)
    field[16 + 8 * n_dir :, :] = jnp.zeros((16, 128), F32)
    totals[...] = jnp.zeros_like(totals)

    def gather_slab(k):
        pltpu.make_async_copy(recv1.at[k], recv1.at[k], recv1_sem.at[k]).wait()
        field[16 : 16 + 8 * n_dir, :] = recv1[k].astype(F32).reshape(8 * n_dir, 128)

        @pl.loop(0, n_dir // 16)
        def _(h):
            acc = [totals[h, i] for i in range(16)]
            for xl in range(2):
                p = 2 * k + xl
                for y in range(6):
                    for z in range(2):
                        rows = [
                            pl.ds((16 * h + y) * 8 + part * 4 + xl * 2 + z, 8, stride=16) for part in range(2)
                        ]
                        targets = [
                            (px, py, pz)
                            for px in range(2) for py in range(2) for pz in range(2)
                            if max(abs(p - 2 - px), abs(y - 2 - py)) > 1
                        ]
                        if not targets:
                            continue
                        re, im = field[rows[0], :], field[rows[1], :]
                        for px, py, pz in targets:
                            at = ((p + 1 - px) * 7 + y + 1 - py) * 6 + (z - pz + 1) * 2
                            fr, fi = factors[at], factors[at + 1]
                            i = (px * 2 + pz) * 2 + py
                            acc[i] = acc[i] + fr * re - fi * im
                            acc[8 + i] = acc[8 + i] + fr * im + fi * re
            for i in range(16):
                totals[h, i] = acc[i]

    gather_slab(1)

    @pl.when(not_first)
    def _():
        gather_slab(0)

    @pl.when(not_last)
    def _():
        gather_slab(2)

    @pl.loop(0, n_dir // 16)
    def _(h):
        for part in range(2):
            for px in range(2):
                for pz in range(2):
                    for py in range(2):
                        row = (16 * h + py) * 8 + part * 4 + px * 2 + pz
                        flat[pl.ds(row, 8, stride=16), :] = totals[h, part * 8 + (px * 2 + pz) * 2 + py]

    send2[...] = flat[...].reshape(n_dir, 8, 128).astype(BF16)

    @pl.loop(1, n_dir)
    def _(k):
        t = lax.rem(d + k, n_dir)
        pltpu.make_async_remote_copy(
            send2.at[t], recv2.at[d], send2_sem, recv2_sem,
            device_id={"dir": t, "slab": s}, device_id_type=MESH,
        ).start()

    pltpu.make_async_copy(send2.at[d], recv2.at[d], recv2_sem).start()
    unsort = selectf[...].T.astype(BF16)
    pltpu.make_async_copy(recv2, recv2, recv2_sem).wait()

    @pl.loop(0, n_dir // 2)
    def _(j):
        cols = pl.ds(pl.multiple_of(j * 128, 128), 128)
        a = recv2[2 * j].astype(F32)
        b = recv2[2 * j + 1].astype(F32)
        e0 = jnp.where(low8, a, pltpu.roll(b, 64, 1))
        e1 = jnp.where(low8, pltpu.roll(a, 64, 1), b)
        x0 = down_sign * pltpu.roll(e0, 4, 0)
        x1 = down_sign * pltpu.roll(e1, 4, 0)
        for q in range(8):
            c, n = cos_t[q : q + 1, cols], sin_t[q : q + 1, cols]
            both = jnp.concatenate([c * e0 + n * x0, c * e1 + n * x1], axis=0)
            split[q * 16 : q * 16 + 16, cols] = both.astype(BF16)

    gathered = scale * lax.dot_general(
        split[...], interp[...], (((1,), (1,)), ((), ())), preferred_element_type=F32
    )
    width = gathered.shape[1]
    blocks = gathered.reshape(16, 8, width)
    swapped = jnp.concatenate([-blocks[:, 4:], blocks[:, :4]], axis=1).reshape(128, width)
    scaled = imp_cols[0, :, 0:1] * gathered + imp_cols[1, :, 0:1] * swapped
    out_ref[...] = jnp.dot(unsort, scaled.astype(BF16), preferred_element_type=F32).astype(BF16)

    pltpu.make_async_copy(send1.at[0 : n_dir - 1], send1.at[0 : n_dir - 1], send1_sem.at[1]).wait()
    pltpu.make_async_copy(send2.at[0 : n_dir - 1], send2.at[0 : n_dir - 1], send2_sem).wait()

    @pl.when(not_first)
    def _():
        pltpu.make_async_copy(send1, send1, send1_sem.at[0]).wait()

    @pl.when(not_last)
    def _():
        pltpu.make_async_copy(send1, send1, send1_sem.at[2]).wait()


def body(child_fields, occupancy, child_octant, shift_angle, interp_matrix, trans_table, impedance):
    n_dir, n_slab = lax.axis_size("dir"), lax.axis_size("slab")
    kc, kp = interp_matrix.shape
    scale = (kc / kp) ** 0.5
    vmem = pl.BlockSpec(memory_space=pltpu.VMEM)
    smem = pl.BlockSpec(memory_space=pltpu.SMEM)
    anywhere = pl.BlockSpec(memory_space=pl.ANY)
    rows = child_fields.reshape(-1, kc)
    out = pl.pallas_call(
        functools.partial(fused, n_dir, n_slab, scale),
        out_shape=jax.ShapeDtypeStruct(rows.shape, BF16),
        in_specs=[vmem, smem, smem, anywhere, anywhere, anywhere, smem],
        out_specs=vmem,
        scratch_shapes=[
            pltpu.VMEM((8, kp), F32),
            pltpu.VMEM((kc, kp), BF16),
            pltpu.VMEM((7, 7, 3, 2, 64), F32),
            pltpu.VMEM((8, kp), F32),
            pltpu.VMEM((8, kp), F32),
            pltpu.VMEM((128, 128), BF16),
            pltpu.VMEM((128, 128), F32),
            pltpu.VMEM((2, 128, 128), F32),
            pltpu.VMEM((128, kp), F32),
            pltpu.VMEM((n_dir, 8, 128), BF16),
            pltpu.VMEM((3, n_dir, 8, 128), BF16),
            pltpu.VMEM((294, 8, 128), F32),
            pltpu.VMEM((8 * n_dir + 32, 128), F32),
            pltpu.VMEM((n_dir // 16, 16, 8, 128), F32),
            pltpu.VMEM((8 * n_dir, 128), F32),
            pltpu.VMEM((n_dir, 8, 128), BF16),
            pltpu.VMEM((n_dir, 8, 128), BF16),
            pltpu.VMEM((128, kp), BF16),
            pltpu.SemaphoreType.DMA((3,)),
            pltpu.SemaphoreType.DMA((3,)),
            pltpu.SemaphoreType.DMA((3,)),
            pltpu.SemaphoreType.DMA,
            pltpu.SemaphoreType.DMA,
        ],
        compiler_params=pltpu.CompilerParams(collective_id=0, has_side_effects=True),
    )(rows, occupancy, child_octant, shift_angle, interp_matrix, trans_table, impedance)
    return out.reshape(child_fields.shape)


def solution(mesh):
    placed = (
        P("slab", "dir", None, None, None, None, None),
        P("slab", "dir", None),
        P("slab", "dir", None, None),
        P(),
        P(),
        P(None, None, None, None, "dir"),
        P("slab", "dir", None, None, None),
    )
    return jax.shard_map(
        body,
        mesh=mesh,
        in_specs=placed,
        out_specs=P("slab", "dir", None, None, None, None, None),
        check_vma=False,
    )
```

```python
import functools

import jax
import jax.numpy as jnp
from jax import lax
from jax.experimental import pallas as pl
from jax.experimental.pallas import tpu as pltpu
from jax.sharding import PartitionSpec as P

MESH = pl.DeviceIdType.MESH
F32 = jnp.float32
BF16 = jnp.bfloat16


def lane_low(shape):
    return lax.broadcasted_iota(jnp.int32, shape, 1) < 64

PLANES = 8
UNTIL = (0, 3, 5, 8)


def fused(
    n_dir, n_slab, scale,
    x_hbm, occ_hbm, oct_hbm, ang_hbm, interp_hbm, table_hbm, imp_hbm,
    out_ref,
    x_in, occ_ref, oct_ref, imp_ref, ang, interp, table, cos_t, sin_t, selectf, imp_cols, spread, send1, recv1,
    real_of, imag_of, field, flat, send2, recv2, split,
    local_sem, send1_sem, recv1_sem, send2_sem, recv2_sem,
):
    d = lax.axis_index("dir")
    s = lax.axis_index("slab")
    not_first = s > 0
    not_last = s < n_slab - 1
    width = n_dir // PLANES
    plane = d // width
    half = n_dir // 2

    loads = [
        pltpu.make_async_copy(a, b, local_sem.at[i])
        for i, (a, b) in enumerate(
            [
                (x_hbm, x_in), (occ_hbm, occ_ref), (oct_hbm, oct_ref), (imp_hbm, imp_ref), (ang_hbm, ang),
                (interp_hbm, interp), (table_hbm.at[:, :, 2:5], table),
            ]
        )
    ]
    for load in loads:
        load.start()

    barrier = pltpu.get_barrier_semaphore()

    @pl.loop(0, n_dir)
    def _(k):
        i = k // width
        ahead = PLANES // 2 + i // 2 - (i % 2) * (1 + 2 * (i // 2))
        t = lax.rem(plane + ahead, PLANES) * width + lax.rem(k + d, width)

        @pl.when(not_first)
        def _():
            pl.semaphore_signal(barrier, inc=1, device_id={"dir": t, "slab": s - 1}, device_id_type=MESH)

        @pl.when(not_last)
        def _():
            pl.semaphore_signal(barrier, inc=1, device_id={"dir": t, "slab": s + 1}, device_id_type=MESH)

        @pl.when(t != d)
        def _():
            pl.semaphore_signal(barrier, inc=1, device_id={"dir": t, "slab": s}, device_id_type=MESH)

    low8 = lane_low((8, 128))
    real8 = lax.broadcasted_iota(jnp.int32, (8, 128), 0) < 4
    up_sign = jnp.where(real8, -1.0, 1.0).astype(F32)
    down_sign = jnp.where(real8, 1.0, -1.0).astype(F32)

    for load in loads[:5]:
        load.wait()
    cos_t[...] = jnp.cos(ang[...])
    sin_t[...] = jnp.sin(ang[...])
    lane = lax.broadcasted_iota(jnp.int32, (1, 128), 1)
    oct_lane = jnp.zeros((1, 128), jnp.int32)
    occ_lane = jnp.zeros((1, 128), F32)
    for box in range(4):
        x, z = box // 2, box % 2
        occ_lane = jnp.where(lane // 32 == box, occ_ref[x, 0, z].astype(F32), occ_lane)
        for slot in range(8):
            oct_lane = jnp.where(lane // 4 == box * 8 + slot, oct_ref[x, 0, z, slot], oct_lane)
    row16 = lax.broadcasted_iota(jnp.int32, (16, 128), 0)
    lane16 = lax.broadcasted_iota(jnp.int32, (16, 128), 1)
    same = (row16 // 8 == (lane16 // 2) % 2) & ((row16 // 4) % 2 == lane16 % 2) & (row16 % 4 == lane16 // 32)
    picked = [jnp.where(same & (oct_lane == q), 1.0, 0.0).astype(F32) for q in range(8)]
    for q in range(8):
        selectf[q * 16 : q * 16 + 16, :] = picked[q]
    select = jnp.concatenate([(p * occ_lane).astype(BF16) for p in picked], axis=0)
    rows_in = x_in[...].reshape(128, x_in.shape[2])
    sorted_x = jnp.dot(select, rows_in, preferred_element_type=F32).astype(BF16)
    loads[5].wait()

    spread[...] = jnp.dot(sorted_x, interp[...], preferred_element_type=F32)

    @pl.loop(0, n_dir // 2, unroll=4)
    def _(j):
        cols = pl.ds(pl.multiple_of(j * 128, 128), 128)
        parts = []
        for e in range(2):
            straight = jnp.zeros((8, 128), F32)
            crossed = jnp.zeros((8, 128), F32)
            for q in range(8):
                v = spread[q * 16 + e * 8 : q * 16 + e * 8 + 8, cols]
                straight += cos_t[q : q + 1, cols] * v
                crossed += sin_t[q : q + 1, cols] * v
            parts.append(straight + up_sign * pltpu.roll(crossed, 4, 0))
        e0, e1 = parts
        send1[2 * j] = jnp.where(low8, e0, pltpu.roll(e1, 64, 1)).astype(BF16)
        send1[2 * j + 1] = jnp.where(low8, pltpu.roll(e0, 64, 1), e1).astype(BF16)

    pl.semaphore_wait(
        barrier, n_dir - 1 + n_dir * (not_first.astype(jnp.int32) + not_last.astype(jnp.int32))
    )

    part = (plane >= UNTIL[1]).astype(jnp.int32) + (plane >= UNTIL[2]).astype(jnp.int32)

    @pl.loop(0, n_dir)
    def _(k):
        t = (PLANES - 1 - k // width) * width + lax.rem(k + d, width)

        @pl.when(not_first)
        def _():
            pltpu.make_async_remote_copy(
                send1.at[t], recv1.at[2, d], send1_sem.at[0], recv1_sem.at[2, part],
                device_id={"dir": t, "slab": s - 1}, device_id_type=MESH,
            ).start()

        @pl.when(not_last)
        def _():
            pltpu.make_async_remote_copy(
                send1.at[t], recv1.at[0, d], send1_sem.at[2], recv1_sem.at[0, part],
                device_id={"dir": t, "slab": s + 1}, device_id_type=MESH,
            ).start()

        @pl.when(t != d)
        def _():
            pltpu.make_async_remote_copy(
                send1.at[t], recv1.at[1, d], send1_sem.at[1], recv1_sem.at[1, part],
                device_id={"dir": t, "slab": s}, device_id_type=MESH,
            ).start()

        @pl.when(t == d)
        def _():
            pltpu.make_async_copy(send1.at[t], recv1.at[1, d], recv1_sem.at[1, part]).start()

    loads[6].wait()
    for a in range(7):
        rows = table[a].reshape(21, 2, 64)
        re, im = rows[:, 0, :], rows[:, 1, :]
        real_of[21 * a : 21 * a + 21, :] = jnp.concatenate([re, re], axis=1)
        imag_of[21 * a : 21 * a + 21, :] = jnp.concatenate([im, im], axis=1)

    imp_re = jnp.zeros((1, 128), F32)
    imp_im = jnp.zeros((1, 128), F32)
    for box in range(4):
        x, z = box // 2, box % 2
        for slot in range(8):
            here = lane // 4 == box * 8 + slot
            imp_re = jnp.where(here, imp_ref[x, 0, z, 0, slot], imp_re)
            imp_im = jnp.where(here, imp_ref[x, 0, z, 1, slot], imp_im)
    for q in range(8):
        row = selectf[q * 16 : q * 16 + 16, :]
        imp_cols[0, q * 16 : q * 16 + 16, :] = jnp.broadcast_to(jnp.sum(row * imp_re, axis=1, keepdims=True), (16, 128))
        imp_cols[1, q * 16 : q * 16 + 16, :] = jnp.broadcast_to(jnp.sum(row * imp_im, axis=1, keepdims=True), (16, 128))
    unsort = selectf[...].T.astype(BF16)

    for k in range(3):
        field[k, 0:16, :] = jnp.zeros((16, 128), F32)
        field[k, 16 + 8 * n_dir :, :] = jnp.zeros((16, 128), F32)

    @pl.when(jnp.logical_not(not_first))
    def _():
        field[0] = jnp.zeros(field.shape[1:], F32)

    @pl.when(jnp.logical_not(not_last))
    def _():
        field[2] = jnp.zeros(field.shape[1:], F32)

    middle = 8 * (UNTIL[2] - UNTIL[1]) * width
    for k in range(3):
        field[k, 16 + 8 * UNTIL[1] * width : 16 + 8 * UNTIL[1] * width + middle, :] = jnp.zeros((middle, 128), F32)

    def arrive(k, item):
        first, count = UNTIL[item] * width, (UNTIL[item + 1] - UNTIL[item]) * width
        block = recv1.at[k, first : first + count]
        pltpu.make_async_copy(block, block, recv1_sem.at[k, item]).wait()
        field[k, 16 + 8 * first : 16 + 8 * (first + count), :] = block[...].astype(F32).reshape(8 * count, 128)

    @pl.loop(0, 3)
    def _(item):
        for i in range(3):
            @pl.when(item == i)
            def _(i=i):
                arrive(1, i)

                @pl.when(not_first)
                def _():
                    arrive(0, i)

                @pl.when(not_last)
                def _():
                    arrive(2, i)

        h = item // 2
        acc = [jnp.zeros((8, 128), F32) for _ in range(16)]
        for p in range(6):
            k, xl = p // 2, p % 2
            for y in range(6):
                for z in range(2):
                    targets = [
                        (px, py, pz)
                        for px in range(2) for py in range(2) for pz in range(2)
                        if max(abs(p - 2 - px), abs(y - 2 - py)) > 1
                    ]
                    if not targets:
                        continue
                    re, im = [
                        field[k, pl.ds((half * h + y) * 8 + c * 4 + xl * 2 + z, 8, stride=16), :] for c in range(2)
                    ]
                    for px, py, pz in targets:
                        at = ((p + 1 - px) * 7 + y + 1 - py) * 3 + z - pz + 1
                        fr, fi = real_of[at : at + 1, :], imag_of[at : at + 1, :]
                        i = (px * 2 + pz) * 2 + py
                        acc[i] = acc[i] + fr * re - fi * im
                        acc[8 + i] = acc[8 + i] + fr * im + fi * re
        for c in range(2):
            for px in range(2):
                for pz in range(2):
                    for py in range(2):
                        row = py * 8 + c * 4 + px * 2 + pz
                        flat[pl.ds(row, 8, stride=16), :] = acc[c * 8 + (px * 2 + pz) * 2 + py]
        quarter = n_dir // 4

        @pl.when(item < 2)
        def _():
            boxes = flat[pl.ds(pl.multiple_of(item * 8 * quarter, 8 * quarter), 8 * quarter), :]
            send2[pl.ds(item * quarter, quarter)] = boxes.reshape(quarter, 8, 128).astype(BF16)

        @pl.when(item == 2)
        def _():
            send2[half:] = flat[...].reshape(half, 8, 128).astype(BF16)

        @pl.loop(0, quarter * (1 + h))
        def _(k):
            t = item * quarter + (k // width) * width + lax.rem(k + d, width)

            @pl.when(t != d)
            def _():
                pltpu.make_async_remote_copy(
                    send2.at[t], recv2.at[d], send2_sem, recv2_sem,
                    device_id={"dir": t, "slab": s}, device_id_type=MESH,
                ).start()

            @pl.when(t == d)
            def _():
                pltpu.make_async_copy(send2.at[t], recv2.at[d], recv2_sem).start()

    pltpu.make_async_copy(recv2, recv2, recv2_sem).wait()

    @pl.loop(0, n_dir // 2, unroll=4)
    def _(j):
        cols = pl.ds(pl.multiple_of(j * 128, 128), 128)
        a = recv2[2 * j].astype(F32)
        b = recv2[2 * j + 1].astype(F32)
        e0 = jnp.where(low8, a, pltpu.roll(b, 64, 1))
        e1 = jnp.where(low8, pltpu.roll(a, 64, 1), b)
        x0 = down_sign * pltpu.roll(e0, 4, 0)
        x1 = down_sign * pltpu.roll(e1, 4, 0)
        for q in range(8):
            c, n = cos_t[q : q + 1, cols], sin_t[q : q + 1, cols]
            both = jnp.concatenate([c * e0 + n * x0, c * e1 + n * x1], axis=0)
            split[q * 16 : q * 16 + 16, cols] = both.astype(BF16)

    gathered = scale * lax.dot_general(
        split[...], interp[...], (((1,), (1,)), ((), ())), preferred_element_type=F32
    )
    across_k = gathered.shape[1]
    blocks = gathered.reshape(16, 8, across_k)
    swapped = jnp.concatenate([-blocks[:, 4:], blocks[:, :4]], axis=1).reshape(128, across_k)
    scaled = imp_cols[0, :, 0:1] * gathered + imp_cols[1, :, 0:1] * swapped
    out_ref[...] = jnp.dot(unsort, scaled.astype(BF16), preferred_element_type=F32).astype(BF16)

    pltpu.make_async_copy(send1.at[0 : n_dir - 1], send1.at[0 : n_dir - 1], send1_sem.at[1]).wait()
    pltpu.make_async_copy(send2.at[0 : n_dir - 1], send2.at[0 : n_dir - 1], send2_sem).wait()

    @pl.when(not_first)
    def _():
        pltpu.make_async_copy(send1, send1, send1_sem.at[0]).wait()

    @pl.when(not_last)
    def _():
        pltpu.make_async_copy(send1, send1, send1_sem.at[2]).wait()


def body(child_fields, occupancy, child_octant, shift_angle, interp_matrix, trans_table, impedance):
    n_dir, n_slab = lax.axis_size("dir"), lax.axis_size("slab")
    kc, kp = interp_matrix.shape
    scale = (kc / kp) ** 0.5
    anywhere = pl.BlockSpec(memory_space=pl.ANY)
    pairs = child_fields.reshape(-1, 2, kc)
    by_part = jnp.swapaxes(impedance, 3, 4)
    out = pl.pallas_call(
        functools.partial(fused, n_dir, n_slab, scale),
        out_shape=jax.ShapeDtypeStruct((2 * pairs.shape[0], kc), BF16),
        in_specs=[anywhere] * 7,
        out_specs=pl.BlockSpec(memory_space=pltpu.VMEM),
        scratch_shapes=[
            pltpu.VMEM(pairs.shape, BF16),
            pltpu.SMEM(occupancy.shape, jnp.int32),
            pltpu.SMEM(child_octant.shape, jnp.int32),
            pltpu.SMEM(by_part.shape, F32),
            pltpu.VMEM((8, kp), F32),
            pltpu.VMEM((kc, kp), BF16),
            pltpu.VMEM((7, 7, 3, 2, 64), F32),
            pltpu.VMEM((8, kp), F32),
            pltpu.VMEM((8, kp), F32),
            pltpu.VMEM((128, 128), F32),
            pltpu.VMEM((2, 128, 128), F32),
            pltpu.VMEM((128, kp), F32),
            pltpu.VMEM((n_dir, 8, 128), BF16),
            pltpu.VMEM((3, n_dir, 8, 128), BF16),
            pltpu.VMEM((152, 128), F32),
            pltpu.VMEM((152, 128), F32),
            pltpu.VMEM((3, 8 * n_dir + 32, 128), F32),
            pltpu.VMEM((4 * n_dir, 128), F32),
            pltpu.VMEM((n_dir, 8, 128), BF16),
            pltpu.VMEM((n_dir, 8, 128), BF16),
            pltpu.VMEM((128, kp), BF16),
            pltpu.SemaphoreType.DMA((7,)),
            pltpu.SemaphoreType.DMA((3,)),
            pltpu.SemaphoreType.DMA((3, 3)),
            pltpu.SemaphoreType.DMA,
            pltpu.SemaphoreType.DMA,
        ],
        compiler_params=pltpu.CompilerParams(collective_id=0, has_side_effects=True),
    )(pairs, occupancy, child_octant, shift_angle, interp_matrix, trans_table, by_part)
    return out.reshape(child_fields.shape)


def solution(mesh):
    placed = (
        P("slab", "dir", None, None, None, None, None),
        P("slab", "dir", None),
        P("slab", "dir", None, None),
        P(),
        P(),
        P(None, None, None, None, "dir"),
        P("slab", "dir", None, None, None),
    )
    return jax.shard_map(
        body,
        mesh=mesh,
        in_specs=placed,
        out_specs=P("slab", "dir", None, None, None, None, None),
        check_vma=False,
    )
```

```python
import functools

import jax
import jax.numpy as jnp
from jax import lax
from jax.experimental import pallas as pl
from jax.experimental.pallas import tpu as pltpu
from jax.sharding import PartitionSpec as P

MESH = pl.DeviceIdType.MESH
F32 = jnp.float32
BF16 = jnp.bfloat16


def lane_low(shape):
    return lax.broadcasted_iota(jnp.int32, shape, 1) < 64

PLANES = 8
UNTIL = (0, 3, 5, 8)


def fused(
    n_dir, n_slab, scale,
    x_hbm, occ_hbm, oct_hbm, ang_hbm, interp_hbm, table_hbm, imp_hbm,
    out_ref,
    x_in, occ_ref, oct_ref, imp_ref, ang, interp, table, cos_t, sin_t, selectf, imp_cols, spread, send1, recv1,
    real_of, imag_of, field, flat, send2, recv2, split, partial_sum,
    local_sem, send1_sem, recv1_sem, send2_sem, recv2_sem,
):
    d = lax.axis_index("dir")
    s = lax.axis_index("slab")
    not_first = s > 0
    not_last = s < n_slab - 1
    width = n_dir // PLANES
    plane = d // width
    half = n_dir // 2

    loads = [
        pltpu.make_async_copy(a, b, local_sem.at[i])
        for i, (a, b) in enumerate(
            [
                (x_hbm, x_in), (occ_hbm, occ_ref), (oct_hbm, oct_ref), (imp_hbm, imp_ref), (ang_hbm, ang),
                (interp_hbm, interp), (table_hbm.at[:, :, 2:5], table),
            ]
        )
    ]
    for load in loads:
        load.start()

    barrier = pltpu.get_barrier_semaphore()

    @pl.loop(0, n_dir)
    def _(k):
        i = k // width
        ahead = PLANES // 2 + i // 2 - (i % 2) * (1 + 2 * (i // 2))
        t = lax.rem(plane + ahead, PLANES) * width + lax.rem(k + d, width)

        @pl.when(not_first)
        def _():
            pl.semaphore_signal(barrier, inc=1, device_id={"dir": t, "slab": s - 1}, device_id_type=MESH)

        @pl.when(not_last)
        def _():
            pl.semaphore_signal(barrier, inc=1, device_id={"dir": t, "slab": s + 1}, device_id_type=MESH)

        @pl.when(t != d)
        def _():
            pl.semaphore_signal(barrier, inc=1, device_id={"dir": t, "slab": s}, device_id_type=MESH)

    low8 = lane_low((8, 128))
    real8 = lax.broadcasted_iota(jnp.int32, (8, 128), 0) < 4
    up_sign = jnp.where(real8, -1.0, 1.0).astype(F32)
    down_sign = jnp.where(real8, 1.0, -1.0).astype(F32)

    for load in loads[:5]:
        load.wait()
    cos_t[...] = jnp.cos(ang[...])
    sin_t[...] = jnp.sin(ang[...])
    lane = lax.broadcasted_iota(jnp.int32, (1, 128), 1)
    oct_lane = jnp.zeros((1, 128), jnp.int32)
    occ_lane = jnp.zeros((1, 128), F32)
    for box in range(4):
        x, z = box // 2, box % 2
        occ_lane = jnp.where(lane // 32 == box, occ_ref[x, 0, z].astype(F32), occ_lane)
        for slot in range(8):
            oct_lane = jnp.where(lane // 4 == box * 8 + slot, oct_ref[x, 0, z, slot], oct_lane)
    row16 = lax.broadcasted_iota(jnp.int32, (16, 128), 0)
    lane16 = lax.broadcasted_iota(jnp.int32, (16, 128), 1)
    same = (row16 // 8 == (lane16 // 2) % 2) & ((row16 // 4) % 2 == lane16 % 2) & (row16 % 4 == lane16 // 32)
    picked = [jnp.where(same & (oct_lane == q), 1.0, 0.0).astype(F32) for q in range(8)]
    for q in range(8):
        selectf[q * 16 : q * 16 + 16, :] = picked[q]
    select = jnp.concatenate([(p * occ_lane).astype(BF16) for p in picked], axis=0)
    rows_in = x_in[...].reshape(128, x_in.shape[2])
    sorted_x = jnp.dot(select, rows_in, preferred_element_type=F32).astype(BF16)
    loads[5].wait()

    spread[...] = jnp.dot(sorted_x, interp[...], preferred_element_type=F32)

    @pl.loop(0, n_dir // 2, unroll=4)
    def _(j):
        cols = pl.ds(pl.multiple_of(j * 128, 128), 128)
        parts = []
        for e in range(2):
            straight = jnp.zeros((8, 128), F32)
            crossed = jnp.zeros((8, 128), F32)
            for q in range(8):
                v = spread[q * 16 + e * 8 : q * 16 + e * 8 + 8, cols]
                straight += cos_t[q : q + 1, cols] * v
                crossed += sin_t[q : q + 1, cols] * v
            parts.append(straight + up_sign * pltpu.roll(crossed, 4, 0))
        e0, e1 = parts
        send1[2 * j] = jnp.where(low8, e0, pltpu.roll(e1, 64, 1)).astype(BF16)
        send1[2 * j + 1] = jnp.where(low8, pltpu.roll(e0, 64, 1), e1).astype(BF16)

    pl.semaphore_wait(
        barrier, n_dir - 1 + n_dir * (not_first.astype(jnp.int32) + not_last.astype(jnp.int32))
    )

    part = (plane >= UNTIL[1]).astype(jnp.int32) + (plane >= UNTIL[2]).astype(jnp.int32)

    @pl.loop(0, n_dir)
    def _(k):
        t = (PLANES - 1 - k // width) * width + lax.rem(k + d, width)

        @pl.when(not_first)
        def _():
            pltpu.make_async_remote_copy(
                send1.at[t], recv1.at[2, d], send1_sem.at[0], recv1_sem.at[2, part],
                device_id={"dir": t, "slab": s - 1}, device_id_type=MESH,
            ).start()

        @pl.when(not_last)
        def _():
            pltpu.make_async_remote_copy(
                send1.at[t], recv1.at[0, d], send1_sem.at[2], recv1_sem.at[0, part],
                device_id={"dir": t, "slab": s + 1}, device_id_type=MESH,
            ).start()

        @pl.when(t != d)
        def _():
            pltpu.make_async_remote_copy(
                send1.at[t], recv1.at[1, d], send1_sem.at[1], recv1_sem.at[1, part],
                device_id={"dir": t, "slab": s}, device_id_type=MESH,
            ).start()

        @pl.when(t == d)
        def _():
            pltpu.make_async_copy(send1.at[t], recv1.at[1, d], recv1_sem.at[1, part]).start()

    loads[6].wait()
    for a in range(7):
        rows = table[a].reshape(21, 2, 64)
        re, im = rows[:, 0, :], rows[:, 1, :]
        real_of[21 * a : 21 * a + 21, :] = jnp.concatenate([re, re], axis=1)
        imag_of[21 * a : 21 * a + 21, :] = jnp.concatenate([im, im], axis=1)

    imp_re = jnp.zeros((1, 128), F32)
    imp_im = jnp.zeros((1, 128), F32)
    for box in range(4):
        x, z = box // 2, box % 2
        for slot in range(8):
            here = lane // 4 == box * 8 + slot
            imp_re = jnp.where(here, imp_ref[x, 0, z, 0, slot], imp_re)
            imp_im = jnp.where(here, imp_ref[x, 0, z, 1, slot], imp_im)
    for q in range(8):
        row = selectf[q * 16 : q * 16 + 16, :]
        imp_cols[0, q * 16 : q * 16 + 16, :] = jnp.broadcast_to(jnp.sum(row * imp_re, axis=1, keepdims=True), (16, 128))
        imp_cols[1, q * 16 : q * 16 + 16, :] = jnp.broadcast_to(jnp.sum(row * imp_im, axis=1, keepdims=True), (16, 128))
    unsort = selectf[...].T.astype(BF16)

    for k in range(3):
        field[k, 0:16, :] = jnp.zeros((16, 128), F32)
        field[k, 16 + 8 * n_dir :, :] = jnp.zeros((16, 128), F32)

    @pl.when(jnp.logical_not(not_first))
    def _():
        field[0] = jnp.zeros(field.shape[1:], F32)

    @pl.when(jnp.logical_not(not_last))
    def _():
        field[2] = jnp.zeros(field.shape[1:], F32)

    middle = 8 * (UNTIL[2] - UNTIL[1]) * width
    for k in range(3):
        field[k, 16 + 8 * UNTIL[1] * width : 16 + 8 * UNTIL[1] * width + middle, :] = jnp.zeros((middle, 128), F32)

    def arrive(k, item):
        first, count = UNTIL[item] * width, (UNTIL[item + 1] - UNTIL[item]) * width
        block = recv1.at[k, first : first + count]
        pltpu.make_async_copy(block, block, recv1_sem.at[k, item]).wait()
        field[k, 16 + 8 * first : 16 + 8 * (first + count), :] = block[...].astype(F32).reshape(8 * count, 128)

    @pl.loop(0, 3)
    def _(item):
        for i in range(3):
            @pl.when(item == i)
            def _(i=i):
                arrive(1, i)

                @pl.when(not_first)
                def _():
                    arrive(0, i)

                @pl.when(not_last)
                def _():
                    arrive(2, i)

        h = item // 2
        acc = [jnp.zeros((8, 128), F32) for _ in range(16)]
        for p in range(6):
            k, xl = p // 2, p % 2
            for y in range(6):
                for z in range(2):
                    targets = [
                        (px, py, pz)
                        for px in range(2) for py in range(2) for pz in range(2)
                        if max(abs(p - 2 - px), abs(y - 2 - py)) > 1
                    ]
                    if not targets:
                        continue
                    re, im = [
                        field[k, pl.ds((half * h + y) * 8 + c * 4 + xl * 2 + z, 8, stride=16), :] for c in range(2)
                    ]
                    for px, py, pz in targets:
                        at = ((p + 1 - px) * 7 + y + 1 - py) * 3 + z - pz + 1
                        fr, fi = real_of[at : at + 1, :], imag_of[at : at + 1, :]
                        i = (px * 2 + pz) * 2 + py
                        acc[i] = acc[i] + fr * re - fi * im
                        acc[8 + i] = acc[8 + i] + fr * im + fi * re
        for c in range(2):
            for px in range(2):
                for pz in range(2):
                    for py in range(2):
                        row = py * 8 + c * 4 + px * 2 + pz
                        flat[pl.ds(row, 8, stride=16), :] = acc[c * 8 + (px * 2 + pz) * 2 + py]
        quarter = n_dir // 4

        @pl.when(item < 2)
        def _():
            boxes = flat[pl.ds(pl.multiple_of(item * 8 * quarter, 8 * quarter), 8 * quarter), :]
            send2[pl.ds(item * quarter, quarter)] = boxes.reshape(quarter, 8, 128).astype(BF16)

        @pl.when(item == 2)
        def _():
            send2[half:] = flat[...].reshape(half, 8, 128).astype(BF16)

        @pl.loop(0, quarter * (1 + h))
        def _(k):
            t = item * quarter + (k // width) * width + lax.rem(k + d, width)

            @pl.when(t != d)
            def _():
                pltpu.make_async_remote_copy(
                    send2.at[t], recv2.at[d], send2_sem, recv2_sem.at[d // half],
                    device_id={"dir": t, "slab": s}, device_id_type=MESH,
                ).start()

            @pl.when(t == d)
            def _():
                pltpu.make_async_copy(send2.at[t], recv2.at[d], recv2_sem.at[d // half]).start()

    def half_back(part):
        replies = recv2.at[half * part : half * part + half]
        pltpu.make_async_copy(replies, replies, recv2_sem.at[part]).wait()

        @pl.loop(part * (half // 2), (part + 1) * (half // 2), unroll=4)
        def _(j):
            cols = pl.ds(pl.multiple_of(j * 128, 128), 128)
            a = recv2[2 * j].astype(F32)
            b = recv2[2 * j + 1].astype(F32)
            e0 = jnp.where(low8, a, pltpu.roll(b, 64, 1))
            e1 = jnp.where(low8, pltpu.roll(a, 64, 1), b)
            x0 = down_sign * pltpu.roll(e0, 4, 0)
            x1 = down_sign * pltpu.roll(e1, 4, 0)
            for q in range(8):
                c, n = cos_t[q : q + 1, cols], sin_t[q : q + 1, cols]
                both = jnp.concatenate([c * e0 + n * x0, c * e1 + n * x1], axis=0)
                split[q * 16 : q * 16 + 16, cols] = both.astype(BF16)

        columns = slice(64 * half * part, 64 * half * (part + 1))
        return lax.dot_general(
            split[:, columns], interp[:, columns], (((1,), (1,)), ((), ())), preferred_element_type=F32
        )

    partial_sum[...] = half_back(0)
    gathered = scale * (partial_sum[...] + half_back(1))
    across_k = gathered.shape[1]
    blocks = gathered.reshape(16, 8, across_k)
    swapped = jnp.concatenate([-blocks[:, 4:], blocks[:, :4]], axis=1).reshape(128, across_k)
    scaled = imp_cols[0, :, 0:1] * gathered + imp_cols[1, :, 0:1] * swapped
    out_ref[...] = jnp.dot(unsort, scaled.astype(BF16), preferred_element_type=F32).astype(BF16)

    pltpu.make_async_copy(send1.at[0 : n_dir - 1], send1.at[0 : n_dir - 1], send1_sem.at[1]).wait()
    pltpu.make_async_copy(send2.at[0 : n_dir - 1], send2.at[0 : n_dir - 1], send2_sem).wait()

    @pl.when(not_first)
    def _():
        pltpu.make_async_copy(send1, send1, send1_sem.at[0]).wait()

    @pl.when(not_last)
    def _():
        pltpu.make_async_copy(send1, send1, send1_sem.at[2]).wait()


def body(child_fields, occupancy, child_octant, shift_angle, interp_matrix, trans_table, impedance):
    n_dir, n_slab = lax.axis_size("dir"), lax.axis_size("slab")
    kc, kp = interp_matrix.shape
    scale = (kc / kp) ** 0.5
    anywhere = pl.BlockSpec(memory_space=pl.ANY)
    pairs = child_fields.reshape(-1, 2, kc)
    by_part = jnp.swapaxes(impedance, 3, 4)
    out = pl.pallas_call(
        functools.partial(fused, n_dir, n_slab, scale),
        out_shape=pltpu.VMEM((2 * pairs.shape[0], kc), BF16),
        in_specs=[anywhere] * 7,
        out_specs=pl.BlockSpec(memory_space=pltpu.VMEM),
        scratch_shapes=[
            pltpu.VMEM(pairs.shape, BF16),
            pltpu.SMEM(occupancy.shape, jnp.int32),
            pltpu.SMEM(child_octant.shape, jnp.int32),
            pltpu.SMEM(by_part.shape, F32),
            pltpu.VMEM((8, kp), F32),
            pltpu.VMEM((kc, kp), BF16),
            pltpu.VMEM((7, 7, 3, 2, 64), F32),
            pltpu.VMEM((8, kp), F32),
            pltpu.VMEM((8, kp), F32),
            pltpu.VMEM((128, 128), F32),
            pltpu.VMEM((2, 128, 128), F32),
            pltpu.VMEM((128, kp), F32),
            pltpu.VMEM((n_dir, 8, 128), BF16),
            pltpu.VMEM((3, n_dir, 8, 128), BF16),
            pltpu.VMEM((152, 128), F32),
            pltpu.VMEM((152, 128), F32),
            pltpu.VMEM((3, 8 * n_dir + 32, 128), F32),
            pltpu.VMEM((4 * n_dir, 128), F32),
            pltpu.VMEM((n_dir, 8, 128), BF16),
            pltpu.VMEM((n_dir, 8, 128), BF16),
            pltpu.VMEM((128, kp), BF16),
            pltpu.VMEM((128, kc), F32),
            pltpu.SemaphoreType.DMA((7,)),
            pltpu.SemaphoreType.DMA((3,)),
            pltpu.SemaphoreType.DMA((3, 3)),
            pltpu.SemaphoreType.DMA,
            pltpu.SemaphoreType.DMA((2,)),
        ],
        compiler_params=pltpu.CompilerParams(collective_id=0, has_side_effects=True),
    )(pairs, occupancy, child_octant, shift_angle, interp_matrix, trans_table, by_part)
    return out.reshape(child_fields.shape)


def solution(mesh):
    placed = (
        P("slab", "dir", None, None, None, None, None),
        P("slab", "dir", None),
        P("slab", "dir", None, None),
        P(),
        P(),
        P(None, None, None, None, "dir"),
        P("slab", "dir", None, None, None),
    )
    return jax.shard_map(
        body,
        mesh=mesh,
        in_specs=placed,
        out_specs=P("slab", "dir", None, None, None, None, None),
        check_vma=False,
    )
```

```python
import functools

import jax
import jax.numpy as jnp
from jax import lax
from jax.experimental import pallas as pl
from jax.experimental.pallas import tpu as pltpu
from jax.sharding import PartitionSpec as P

MESH = pl.DeviceIdType.MESH
F32 = jnp.float32
BF16 = jnp.bfloat16


def lane_low(shape):
    return lax.broadcasted_iota(jnp.int32, shape, 1) < 64

PLANES = 8
UNTIL = (0, 3, 5, 8)


def fused(
    n_dir, n_slab, scale,
    x_hbm, occ_hbm, oct_hbm, ang_hbm, interp_hbm, table_hbm, imp_hbm,
    out_ref,
    x_in, occ_ref, oct_ref, imp_ref, ang, interp, table, cos_t, sin_t, selectf, imp_cols, spread, send1, recv1,
    real_of, imag_of, field, flat, send2, recv2, split, partial_sum,
    local_sem, send1_sem, recv1_sem, send2_sem, recv2_sem,
):
    d = lax.axis_index("dir")
    s = lax.axis_index("slab")
    not_first = s > 0
    not_last = s < n_slab - 1
    width = n_dir // PLANES
    plane = d // width
    half = n_dir // 2

    loads = [
        pltpu.make_async_copy(a, b, local_sem.at[i])
        for i, (a, b) in enumerate(
            [
                (x_hbm, x_in), (occ_hbm, occ_ref), (oct_hbm, oct_ref), (imp_hbm, imp_ref), (ang_hbm, ang),
                (interp_hbm, interp), (table_hbm.at[:, :, 2:5], table),
            ]
        )
    ]
    for load in loads:
        load.start()

    barrier = pltpu.get_barrier_semaphore()

    @pl.loop(0, n_dir)
    def _(k):
        i = k // width
        ahead = PLANES // 2 + i // 2 - (i % 2) * (1 + 2 * (i // 2))
        t = lax.rem(plane + ahead, PLANES) * width + lax.rem(k + d, width)

        @pl.when(not_first)
        def _():
            pl.semaphore_signal(barrier, inc=1, device_id={"dir": t, "slab": s - 1}, device_id_type=MESH)

        @pl.when(not_last)
        def _():
            pl.semaphore_signal(barrier, inc=1, device_id={"dir": t, "slab": s + 1}, device_id_type=MESH)

        @pl.when(t != d)
        def _():
            pl.semaphore_signal(barrier, inc=1, device_id={"dir": t, "slab": s}, device_id_type=MESH)

    low8 = lane_low((8, 128))
    real8 = lax.broadcasted_iota(jnp.int32, (8, 128), 0) < 4
    up_sign = jnp.where(real8, -1.0, 1.0).astype(F32)
    down_sign = jnp.where(real8, 1.0, -1.0).astype(F32)

    for load in loads[:5]:
        load.wait()
    cos_t[...] = jnp.cos(ang[...])
    sin_t[...] = jnp.sin(ang[...])
    lane = lax.broadcasted_iota(jnp.int32, (1, 128), 1)
    oct_lane = jnp.zeros((1, 128), jnp.int32)
    occ_lane = jnp.zeros((1, 128), F32)
    for box in range(4):
        x, z = box // 2, box % 2
        occ_lane = jnp.where(lane // 32 == box, occ_ref[x, 0, z].astype(F32), occ_lane)
        for slot in range(8):
            oct_lane = jnp.where(lane // 4 == box * 8 + slot, oct_ref[x, 0, z, slot], oct_lane)
    row16 = lax.broadcasted_iota(jnp.int32, (16, 128), 0)
    lane16 = lax.broadcasted_iota(jnp.int32, (16, 128), 1)
    same = (row16 // 8 == (lane16 // 2) % 2) & ((row16 // 4) % 2 == lane16 % 2) & (row16 % 4 == lane16 // 32)
    picked = [jnp.where(same & (oct_lane == q), 1.0, 0.0).astype(F32) for q in range(8)]
    for q in range(8):
        selectf[q * 16 : q * 16 + 16, :] = picked[q]
    select = jnp.concatenate([(p * occ_lane).astype(BF16) for p in picked], axis=0)
    rows_in = x_in[...].reshape(128, x_in.shape[2])
    sorted_x = jnp.dot(select, rows_in, preferred_element_type=F32).astype(BF16)
    loads[5].wait()

    spread[...] = jnp.dot(sorted_x, interp[...], preferred_element_type=F32)

    @pl.loop(0, n_dir // 2, unroll=4)
    def _(j):
        cols = pl.ds(pl.multiple_of(j * 128, 128), 128)
        parts = []
        for e in range(2):
            straight = jnp.zeros((8, 128), F32)
            crossed = jnp.zeros((8, 128), F32)
            for q in range(8):
                v = spread[q * 16 + e * 8 : q * 16 + e * 8 + 8, cols]
                straight += cos_t[q : q + 1, cols] * v
                crossed += sin_t[q : q + 1, cols] * v
            parts.append(straight + up_sign * pltpu.roll(crossed, 4, 0))
        e0, e1 = parts
        send1[2 * j] = jnp.where(low8, e0, pltpu.roll(e1, 64, 1)).astype(BF16)
        send1[2 * j + 1] = jnp.where(low8, pltpu.roll(e0, 64, 1), e1).astype(BF16)

    pl.semaphore_wait(
        barrier, n_dir - 1 + n_dir * (not_first.astype(jnp.int32) + not_last.astype(jnp.int32))
    )

    part = (plane >= UNTIL[1]).astype(jnp.int32) + (plane >= UNTIL[2]).astype(jnp.int32)

    @pl.loop(0, n_dir)
    def _(k):
        t = (PLANES - 1 - k // width) * width + lax.rem(k + d, width)

        @pl.when(not_first)
        def _():
            pltpu.make_async_remote_copy(
                send1.at[t], recv1.at[2, d], send1_sem.at[0], recv1_sem.at[2, part],
                device_id={"dir": t, "slab": s - 1}, device_id_type=MESH,
            ).start()

        @pl.when(not_last)
        def _():
            pltpu.make_async_remote_copy(
                send1.at[t], recv1.at[0, d], send1_sem.at[2], recv1_sem.at[0, part],
                device_id={"dir": t, "slab": s + 1}, device_id_type=MESH,
            ).start()

        @pl.when(t != d)
        def _():
            pltpu.make_async_remote_copy(
                send1.at[t], recv1.at[1, d], send1_sem.at[1], recv1_sem.at[1, part],
                device_id={"dir": t, "slab": s}, device_id_type=MESH,
            ).start()

        @pl.when(t == d)
        def _():
            pltpu.make_async_copy(send1.at[t], recv1.at[1, d], recv1_sem.at[1, part]).start()

    loads[6].wait()
    for a in range(7):
        rows = table[a].reshape(21, 2, 64)
        re, im = rows[:, 0, :], rows[:, 1, :]
        real_of[21 * a : 21 * a + 21, :] = jnp.concatenate([re, re], axis=1)
        imag_of[21 * a : 21 * a + 21, :] = jnp.concatenate([im, im], axis=1)

    imp_re = jnp.zeros((1, 128), F32)
    imp_im = jnp.zeros((1, 128), F32)
    for box in range(4):
        x, z = box // 2, box % 2
        for slot in range(8):
            here = lane // 4 == box * 8 + slot
            imp_re = jnp.where(here, imp_ref[x, 0, z, 0, slot], imp_re)
            imp_im = jnp.where(here, imp_ref[x, 0, z, 1, slot], imp_im)
    for q in range(8):
        row = selectf[q * 16 : q * 16 + 16, :]
        imp_cols[0, q * 16 : q * 16 + 16, :] = jnp.broadcast_to(jnp.sum(row * imp_re, axis=1, keepdims=True), (16, 128))
        imp_cols[1, q * 16 : q * 16 + 16, :] = jnp.broadcast_to(jnp.sum(row * imp_im, axis=1, keepdims=True), (16, 128))
    unsort = selectf[...].T.astype(BF16)

    for k in range(3):
        field[k, 0:16, :] = jnp.zeros((16, 128), F32)
        field[k, 16 + 8 * n_dir :, :] = jnp.zeros((16, 128), F32)

    @pl.when(jnp.logical_not(not_first))
    def _():
        field[0] = jnp.zeros(field.shape[1:], F32)

    @pl.when(jnp.logical_not(not_last))
    def _():
        field[2] = jnp.zeros(field.shape[1:], F32)

    middle = 8 * (UNTIL[2] - UNTIL[1]) * width
    for k in range(3):
        field[k, 16 + 8 * UNTIL[1] * width : 16 + 8 * UNTIL[1] * width + middle, :] = jnp.zeros((middle, 128), F32)

    def arrive(k, item):
        first, count = UNTIL[item] * width, (UNTIL[item + 1] - UNTIL[item]) * width
        block = recv1.at[k, first : first + count]
        pltpu.make_async_copy(block, block, recv1_sem.at[k, item]).wait()
        field[k, 16 + 8 * first : 16 + 8 * (first + count), :] = block[...].astype(F32).reshape(8 * count, 128)

    @pl.loop(0, 3)
    def _(item):
        for i in range(3):
            @pl.when(item == i)
            def _(i=i):
                arrive(1, i)

                @pl.when(not_first)
                def _():
                    arrive(0, i)

                @pl.when(not_last)
                def _():
                    arrive(2, i)

        h = item // 2
        acc = [jnp.zeros((8, 128), F32) for _ in range(16)]
        for p in range(6):
            k, xl = p // 2, p % 2
            for y in range(6):
                for z in range(2):
                    targets = [
                        (px, py, pz)
                        for px in range(2) for py in range(2) for pz in range(2)
                        if max(abs(p - 2 - px), abs(y - 2 - py)) > 1
                    ]
                    if not targets:
                        continue
                    re, im = [
                        field[k, pl.ds((half * h + y) * 8 + c * 4 + xl * 2 + z, 8, stride=16), :] for c in range(2)
                    ]
                    for px, py, pz in targets:
                        at = ((p + 1 - px) * 7 + y + 1 - py) * 3 + z - pz + 1
                        fr, fi = real_of[at : at + 1, :], imag_of[at : at + 1, :]
                        i = (px * 2 + pz) * 2 + py
                        acc[i] = acc[i] + fr * re - fi * im
                        acc[8 + i] = acc[8 + i] + fr * im + fi * re
        for c in range(2):
            for px in range(2):
                for pz in range(2):
                    for py in range(2):
                        row = py * 8 + c * 4 + px * 2 + pz
                        flat[pl.ds(row, 8, stride=16), :] = acc[c * 8 + (px * 2 + pz) * 2 + py]
        quarter = n_dir // 4

        @pl.when(item < 2)
        def _():
            boxes = flat[pl.ds(pl.multiple_of(item * 8 * quarter, 8 * quarter), 8 * quarter), :]
            send2[pl.ds(item * quarter, quarter)] = boxes.reshape(quarter, 8, 128).astype(BF16)

        @pl.when(item == 2)
        def _():
            send2[half:] = flat[...].reshape(half, 8, 128).astype(BF16)

        @pl.loop(0, quarter * (1 + h))
        def _(k):
            t = item * quarter + (k // width) * width + lax.rem(k + d, width)

            @pl.when(t != d)
            def _():
                pltpu.make_async_remote_copy(
                    send2.at[t], recv2.at[d], send2_sem, recv2_sem.at[d // half],
                    device_id={"dir": t, "slab": s}, device_id_type=MESH,
                ).start()

            @pl.when(t == d)
            def _():
                pltpu.make_async_copy(send2.at[t], recv2.at[d], recv2_sem.at[d // half]).start()

    def half_back(part):
        replies = recv2.at[half * part : half * part + half]
        pltpu.make_async_copy(replies, replies, recv2_sem.at[part]).wait()

        @pl.loop(part * (half // 2), (part + 1) * (half // 2), unroll=4)
        def _(j):
            cols = pl.ds(pl.multiple_of(j * 128, 128), 128)
            a = recv2[2 * j].astype(F32)
            b = recv2[2 * j + 1].astype(F32)
            e0 = jnp.where(low8, a, pltpu.roll(b, 64, 1))
            e1 = jnp.where(low8, pltpu.roll(a, 64, 1), b)
            x0 = down_sign * pltpu.roll(e0, 4, 0)
            x1 = down_sign * pltpu.roll(e1, 4, 0)
            for q in range(8):
                c, n = cos_t[q : q + 1, cols], sin_t[q : q + 1, cols]
                both = jnp.concatenate([c * e0 + n * x0, c * e1 + n * x1], axis=0)
                split[q * 16 : q * 16 + 16, cols] = both.astype(BF16)

        columns = slice(64 * half * part, 64 * half * (part + 1))
        return lax.dot_general(
            split[:, columns], interp[:, columns], (((1,), (1,)), ((), ())), preferred_element_type=F32
        )

    partial_sum[...] = half_back(0)
    gathered = scale * (partial_sum[...] + half_back(1))
    across_k = gathered.shape[1]
    blocks = gathered.reshape(16, 8, across_k)
    swapped = jnp.concatenate([-blocks[:, 4:], blocks[:, :4]], axis=1).reshape(128, across_k)
    scaled = imp_cols[0, :, 0:1] * gathered + imp_cols[1, :, 0:1] * swapped
    result = jnp.dot(unsort, scaled.astype(BF16), preferred_element_type=F32).astype(BF16)
    out_ref[...] = result.reshape(out_ref.shape)

    pltpu.make_async_copy(send1.at[0 : n_dir - 1], send1.at[0 : n_dir - 1], send1_sem.at[1]).wait()
    pltpu.make_async_copy(send2.at[0 : n_dir - 1], send2.at[0 : n_dir - 1], send2_sem).wait()

    @pl.when(not_first)
    def _():
        pltpu.make_async_copy(send1, send1, send1_sem.at[0]).wait()

    @pl.when(not_last)
    def _():
        pltpu.make_async_copy(send1, send1, send1_sem.at[2]).wait()


def body(child_fields, occupancy, child_octant, shift_angle, interp_matrix, trans_table, impedance):
    n_dir, n_slab = lax.axis_size("dir"), lax.axis_size("slab")
    kc, kp = interp_matrix.shape
    scale = (kc / kp) ** 0.5
    anywhere = pl.BlockSpec(memory_space=pl.ANY)
    pairs = child_fields.reshape(-1, 2, kc)
    by_part = jnp.swapaxes(impedance, 3, 4)
    out = pl.pallas_call(
        functools.partial(fused, n_dir, n_slab, scale),
        out_shape=pltpu.VMEM(pairs.shape, BF16),
        in_specs=[anywhere] * 7,
        out_specs=pl.BlockSpec(memory_space=pltpu.VMEM),
        scratch_shapes=[
            pltpu.VMEM(pairs.shape, BF16),
            pltpu.SMEM(occupancy.shape, jnp.int32),
            pltpu.SMEM(child_octant.shape, jnp.int32),
            pltpu.SMEM(by_part.shape, F32),
            pltpu.VMEM((8, kp), F32),
            pltpu.VMEM((kc, kp), BF16),
            pltpu.VMEM((7, 7, 3, 2, 64), F32),
            pltpu.VMEM((8, kp), F32),
            pltpu.VMEM((8, kp), F32),
            pltpu.VMEM((128, 128), F32),
            pltpu.VMEM((2, 128, 128), F32),
            pltpu.VMEM((128, kp), F32),
            pltpu.VMEM((n_dir, 8, 128), BF16),
            pltpu.VMEM((3, n_dir, 8, 128), BF16),
            pltpu.VMEM((152, 128), F32),
            pltpu.VMEM((152, 128), F32),
            pltpu.VMEM((3, 8 * n_dir + 32, 128), F32),
            pltpu.VMEM((4 * n_dir, 128), F32),
            pltpu.VMEM((n_dir, 8, 128), BF16),
            pltpu.VMEM((n_dir, 8, 128), BF16),
            pltpu.VMEM((128, kp), BF16),
            pltpu.VMEM((128, kc), F32),
            pltpu.SemaphoreType.DMA((7,)),
            pltpu.SemaphoreType.DMA((3,)),
            pltpu.SemaphoreType.DMA((3, 3)),
            pltpu.SemaphoreType.DMA,
            pltpu.SemaphoreType.DMA((2,)),
        ],
        compiler_params=pltpu.CompilerParams(collective_id=0, has_side_effects=True),
    )(pairs, occupancy, child_octant, shift_angle, interp_matrix, trans_table, by_part)
    return out.reshape(child_fields.shape)


def solution(mesh):
    placed = (
        P("slab", "dir", None, None, None, None, None),
        P("slab", "dir", None),
        P("slab", "dir", None, None),
        P(),
        P(),
        P(None, None, None, None, "dir"),
        P("slab", "dir", None, None, None),
    )
    return jax.shard_map(
        body,
        mesh=mesh,
        in_specs=placed,
        out_specs=P("slab", "dir", None, None, None, None, None),
        check_vma=False,
    )
```
